128 devices in a mesh: dp: 16 (over x, y), expert: 8 (over z, core).
Axes of the slice: x: 4, y: 4, z: 4, core: 2. Of those that a mesh axis runs over, the one named last changes fastest.
Arguments:
- tokens: bfloat16 [2048, 6144], P('dp'), may hold values from -6 to 6
- routes: int32 [2048, 2], P('dp'), may hold values from 0 to 7, all different within a row; in each aligned block of 128 rows (0 to 127, 128 to 255, ...) at most 64 rows name the same one
- gates: float32 [2048, 2], P('dp'), may hold values from 0.1 to 1
- capacity: int32 [8], replicated, may hold values from 32 to 64, as said below
- w_gate: bfloat16 [8, 6144, 8192], P('expert', None, 'dp'), may hold values from -0.078125 to 0.078125
- w_up: bfloat16 [8, 6144, 8192], P('expert', None, 'dp'), may hold values from -0.078125 to 0.078125
- w_down: bfloat16 [8, 8192, 6144], P('expert', 'dp'), may hold values from -0.0625 to 0.0625
Outputs:
- mixed: bfloat16 [2048, 6144], P('dp', 'expert')
The draws below stay inside these ranges and needn't reach their ends.
Inputs may be any that keep to these rules, and one draw needn't show every extreme that they name: `routes`: each token names two different experts. Within the 128 tokens of one index of dp no expert is named by more than 64 tokens, and in some shards one expert is named by exactly 64. Some expert's capacity is exactly 64.
All inputs are finite; a program needn't handle non-finite values.
Results may differ from the reference program's by a relative error of at most 0.015.
Values may be sent and summed in bfloat16 or wider, within the bound.
No kernel may reach another device: no remote copies, remote signals or barrier semaphores. Data moves between devices by JAX's collectives and lax.ppermute only.
A program may use at most 128 MiB of HBM per device.

```python
import math
import jax
import jax.numpy as jnp
import numpy as np
from jax import lax

D = 6144
FF = 8192
TOK_DP = 128
EXPERTS = 8
CAP = 64
TOKENS = 2048
N_DP = 16


def draw_capacity(key, part):
    values = jax.random.randint(key, (EXPERTS,), CAP // 2, CAP + 1)
    picked = jax.random.randint(jax.random.fold_in(key, 7), (), 0, EXPERTS)
    return jnp.where(jnp.arange(EXPERTS) == picked, CAP, values).astype(jnp.int32)


def shard_levels(rng, extent, cuts, least, high):
    loudness = 1.0
    for dim, parts in cuts:
        draws = jax.random.uniform(jax.random.fold_in(jax.random.fold_in(rng, 6), dim), (parts,), jnp.float32, least / len(cuts), high / len(cuts))
        loudness = loudness * jnp.repeat(jnp.exp(draws), extent[dim] // parts).reshape((-1,) + (1,) * (len(extent) - 1 - dim))
    return loudness


def routed_block(own_key, own, number, rows, number_of, top, limit, lean):
    order = jax.random.permutation(own_key, number_of)
    packed, ordinary = load_shares(number_of, rows * top, limit, lean, True), load_shares(number_of, rows * top, limit, lean, False)
    places = jnp.arange(number_of)

    def named(sizes, turn):
        used = int((sizes > 0).sum())
        fixed = max(1, used // 4)
        shifted = fixed + (places - fixed + turn * (used - fixed)) % max(1, number_of - fixed)
        return jnp.zeros((number_of,), jnp.int32).at[order[jnp.where(places < fixed, places, shifted)]].set(jnp.asarray(sizes, jnp.int32))

    sizes = jnp.where(number % 4 == 0, named(packed, number // 4), named(ordinary, number - number // 4 - 1))
    mixed = jax.random.permutation(jax.random.fold_in(own, 3), number_of)
    source_of, taker = mixed[0:number_of // 2 * 2:2], mixed[1:number_of // 2 * 2:2]
    slack = jnp.minimum(sizes[source_of] - 1, limit - sizes[taker]) // 2
    slack = jnp.where((source_of == order[0]) | (taker == order[0]) | (sizes[taker] == 0), 0, jnp.maximum(slack, 0))
    shifted = jax.random.randint(jax.random.fold_in(own, 4), (number_of // 2,), 0, 1 << 20) % (slack + 1)
    sizes = sizes.at[source_of].add(-shifted).at[taker].add(shifted)
    items = jnp.searchsorted(jnp.cumsum(sizes), jnp.arange(rows * top), side="right").astype(jnp.int32)
    table = items.reshape(top, rows).T
    table = table[jax.random.permutation(jax.random.fold_in(own, 1), rows)]
    turn = jax.random.randint(jax.random.fold_in(own, 2), (rows, 1), 0, top)
    return jnp.take_along_axis(table, (jnp.arange(top)[None, :] + turn) % top, axis=1)


def load_shares(amount, total, reach, slope, full):
    portions = [(1 << 20) // math.isqrt(rank ** slope) + 1 for rank in range(1, amount + 1)]
    largest = reach if full else min(reach, max(-(-total // amount), total * portions[0] // sum(portions)))
    least = 1 if total - largest >= amount - 1 else 0
    given, rest = [largest] + [least] * (amount - 1), total - largest - least * (amount - 1)
    while rest > 0:
        candidates = [i for i in range(1, amount) if given[i] < largest] or [i for i in range(1, amount) if given[i] < reach]
        mass, remaining = sum([portions[i] for i in candidates]), rest
        for i in candidates:
            extra = min(reach - given[i], max(1, remaining * portions[i] // mass), rest)
            given[i] = given[i] + extra
            rest = rest - extra
    return np.array(given)


def noise(rng, shape, deviation, bound, cuts=(), kind=jnp.bfloat16):
    gain = shard_levels(rng, shape, cuts, -0.22, 0.18) if cuts else 1.0
    array = jax.random.normal(rng, shape, jnp.float32) * deviation * gain
    return jnp.minimum(jnp.maximum(array, -bound), bound).astype(kind)


def setup_inputs(seed: int = 0) -> dict:
    key_list = jax.random.split(jax.random.key(seed), 8)
    tokens = noise(key_list[0], (TOKENS, D), 1.0, 6.0, ((0, 16),))
    routes_keys = jax.random.split(jax.random.fold_in(key_list[1], 1), TOKENS // TOK_DP)
    routes_turns = jax.random.permutation(jax.random.fold_in(key_list[1], 3), TOKENS // TOK_DP)
    routes = jax.vmap(lambda own, number: routed_block(jax.random.fold_in(key_list[1], 2), own, number, TOK_DP, EXPERTS, 2, CAP, 2))(routes_keys, routes_turns).reshape((TOKENS, 2))
    gates = jnp.clip(0.1 + 0.9 * jax.random.uniform(key_list[2], (TOKENS, 2), jnp.float32) ** shard_levels(key_list[2], (TOKENS, 2), ((0, 16),), -0.2, 0.2), 0.1, 1.0)
    capacity = draw_capacity(jax.random.fold_in(key_list[7], 71), 0)
    w_gate = noise(key_list[4], (EXPERTS, D, FF), D ** -0.5, 0.078125, ((0, 8), (2, 16)))
    w_up = noise(key_list[5], (EXPERTS, D, FF), D ** -0.5, 0.078125, ((0, 8), (2, 16)))
    w_down = noise(key_list[6], (EXPERTS, FF, D), FF ** -0.5, 0.0625, ((0, 8), (1, 16)))
    return dict(tokens=tokens, routes=routes, gates=gates, capacity=capacity, w_gate=w_gate, w_up=w_up, w_down=w_down)


def reference(tokens, routes, gates, capacity, w_gate, w_up, w_down):
    shards = tokens.reshape(N_DP, TOK_DP, D)
    chosen = routes.reshape(N_DP, TOK_DP, 2)
    weights_all = gates.reshape(N_DP, TOK_DP, 2)
    slot_ids = jnp.arange(CAP, dtype=jnp.int32)
    panel_width = FF // N_DP
    accumulated = jnp.zeros((N_DP, TOK_DP, D), jnp.float32)
    for expert_id in range(EXPERTS):
        matched = chosen == expert_id
        member = jnp.any(matched, axis=-1).astype(jnp.int32)
        weight = jnp.sum(jnp.where(matched, weights_all, 0.0), axis=-1).astype(jnp.float32)
        position = jnp.cumsum(member, axis=1).astype(jnp.int32) - member
        retained = (member == 1) & (position < capacity[expert_id])
        selector = (retained[:, None, :] & (position[:, None, :] == slot_ids[None, :, None])).astype(jnp.float32)
        slot_rows = jnp.einsum("nct,ntd->ncd", selector, shards.astype(jnp.float32),
                               precision=lax.Precision.HIGHEST).astype(jnp.bfloat16)
        flat_rows = slot_rows.reshape(N_DP * CAP, D)
        gate_act = jnp.dot(flat_rows, w_gate[expert_id], preferred_element_type=jnp.float32)
        up_act = jnp.dot(flat_rows, w_up[expert_id], preferred_element_type=jnp.float32)
        hidden = (jax.nn.silu(gate_act) * up_act).astype(jnp.bfloat16)
        expert_out = jnp.zeros((N_DP * CAP, D), jnp.float32)
        for panel in range(N_DP):
            partial_value = jnp.dot(hidden[:, panel * panel_width:(panel + 1) * panel_width],
                              w_down[expert_id, panel * panel_width:(panel + 1) * panel_width, :],
                              preferred_element_type=jnp.float32).astype(jnp.bfloat16)
            partial_value = lax.optimization_barrier(partial_value)
            expert_out = expert_out + partial_value.astype(jnp.float32)
        placed = jnp.einsum("nct,ncd->ntd", selector, expert_out.reshape(N_DP, CAP, D),
                            precision=lax.Precision.HIGHEST)
        accumulated = accumulated + weight[:, :, None] * placed
    return accumulated.reshape(TOKENS, D).astype(jnp.bfloat16)
```

```python
import jax
import jax.numpy as jnp
from jax import lax
from jax.experimental import pallas as pl
from jax.experimental.pallas import tpu as pltpu
from jax.sharding import PartitionSpec as P


SIDE = 4
CORES = 2
F32 = jnp.float32
BF16 = jnp.bfloat16
STEPS = 4


def move(value, route):
    pairs = []
    for device in range(SIDE * SIDE * SIDE * CORES):
        rest, core = divmod(device, CORES)
        rest, z = divmod(rest, SIDE)
        x, y = divmod(rest, SIDE)
        x, y, z, core = route(x, y, z, core)
        pairs.append((device, ((x % SIDE * SIDE + y % SIDE) * SIDE + z % SIDE) * CORES + core))
    return lax.ppermute(value, ("dp", "expert"), pairs)


def hop(value, leg, step):
    def route(x, y, z, core):
        if core == leg:
            return x + step, y, z, core
        return x, y + step, z, core

    return move(value, route)


def hop_z(value, step):
    return move(value, lambda x, y, z, core: (x, y, z + step, core))


def swap(value):
    return move(value, lambda x, y, z, core: (x, y, z, 1 - core))


def ring_gather(block, leg):
    half = block.shape[0] // 2
    before = hop(block, leg, 1)
    after = hop(block, leg, -1)
    far_low = hop(before[:half], leg, 1)
    far_high = hop(after[half:], leg, -1)
    return before, after, far_low, far_high


def add(first, *others):
    total = first.astype(F32)
    for other in others:
        total = total + other.astype(F32)
    return total


def ring_scatter(own, before, after, far, leg):
    low_after = hop(before[1], leg, -1)
    low_before = hop(after[0], leg, 1)
    low = hop(far[0], leg, -1)
    high = hop(far[1], leg, 1)
    from_after = hop(add(before[0], low).astype(BF16), leg, -1)
    from_before = hop(add(after[1], high).astype(BF16), leg, 1)
    return own[0], low_before, from_after, own[1], low_after, from_before


def vmem_call(kernel, outs, *args, scalars=0, blocks=0, limit=20):
    specs = [pl.BlockSpec(memory_space=pltpu.SMEM)] * scalars
    specs += [pl.BlockSpec(memory_space=pltpu.VMEM)] * (len(args) - scalars - blocks)
    specs += [pl.BlockSpec()] * blocks
    space = pl.BlockSpec(memory_space=pltpu.VMEM) if limit < 50 else pl.BlockSpec()
    return pl.pallas_call(
        kernel,
        in_specs=specs,
        out_specs=[space] * len(outs),
        out_shape=[jax.ShapeDtypeStruct(shape, dtype) for shape, dtype in outs],
        compiler_params=pltpu.CompilerParams(vmem_limit_bytes=limit * 2**20),
    )(*args)


def line_kernel(*refs):
    chains, (minus, plus, near_minus, near_plus, own) = (refs[:6], refs[6:12]), refs[12:]
    tile = 512
    q = near_minus.shape[0] // 2

    @pl.loop(0, minus.shape[1] // tile)
    def _(i):
        at = pl.ds(pl.multiple_of(i * tile, tile), tile)
        for k, (own_low, low_before, from_after, own_high, low_after, from_before) in enumerate(chains):
            low = add(own_low[:, at], low_before[:, at], from_after[:, at])
            high = add(own_high[:, at], low_after[:, at], from_before[:, at])

            def put(out, row, value):
                out[pl.ds(row + k * q, q), at] = value.astype(out.dtype)

            put(own, 0, low[:q])
            put(own, 2 * q, low[q:2 * q])
            put(near_minus, 0, low[2 * q:3 * q])
            put(minus, 2 * q, low[3 * q:])
            put(plus, 2 * q, high[:q])
            put(near_plus, 0, high[q:2 * q])
            put(minus, 0, high[2 * q:3 * q])
            put(plus, 0, high[3 * q:])


def sum_kernel(place, own, from_minus, from_plus, near_after, near_before, mine, theirs):
    half = near_after.shape[0]
    q = half // 2
    width = mine.shape[1] // SIDE

    @pl.loop(0, SIDE)
    def _(k):
        to = pl.ds(pl.multiple_of(k * width, width), width)
        for core, out in ((place[1], mine), (1 - place[1], theirs)):
            at = pl.ds(pl.multiple_of((CORES * k + core) * width, width), width)
            first = add(own[:half, at], from_plus[half:, at], near_after[:, at]).astype(BF16)
            second = add(own[half:, at], from_minus[half:, at], near_before[:, at]).astype(BF16)
            out[:, to] = jnp.concatenate([first[:q], second[:q], first[q:], second[q:]], 0)


def spread_kernel(place, mine, theirs, picks, weights, *outs):
    half = mine.shape[0] // 2
    width = outs[0].shape[1]
    for step, out in enumerate(outs):
        at = pl.ds(pl.multiple_of((place[0] + step) % SIDE * width, width), width)
        total = 0.0
        for e in range(2):
            rows = [mine[e * half:(e + 1) * half, at], theirs[(1 - e) * half:(2 - e) * half, at]]
            value = jnp.dot(picks[e], jnp.concatenate(rows, 0), preferred_element_type=F32)
            total = total + weights[:, e:e + 1] * value
        out[...] = total.astype(out.dtype)


def final_kernel(own, *refs):
    refs[-1][...] = add(own[...], *[ref[...] for ref in refs[:-1]]).astype(BF16)


def ffn_kernel(n, *refs):
    pieces, (w_gate, w_up, w_down) = refs[:n], refs[n:n + 3]
    outs, (gate_sum, up_sum, hidden) = refs[n + 3:-3], refs[-3:]
    i = pl.program_id(0)

    @pl.when(i < STEPS)
    def _():
        block = jnp.concatenate([piece[...] for piece in pieces], 0)
        tile = block.shape[1]
        at = pl.ds(pl.multiple_of(i * tile, tile), tile)
        gate_value = jnp.dot(block, w_gate[0, at], preferred_element_type=F32)
        up_value = jnp.dot(block, w_up[0, at], preferred_element_type=F32)

        @pl.when(i == 0)
        def _():
            gate_sum[...] = gate_value
            up_sum[...] = up_value

        @pl.when(i > 0)
        def _():
            gate_sum[...] += gate_value
            up_sum[...] += up_value

        @pl.when(i == STEPS - 1)
        def _():
            hidden[...] = (jax.nn.silu(gate_sum[...]) * up_sum[...]).astype(BF16)

    @pl.when(i >= STEPS)
    def _():
        tile = outs[0].shape[1]
        cols = pl.ds(pl.multiple_of((i - STEPS) * tile, tile), tile)
        value = jnp.dot(hidden[...], w_down[0, :, cols], preferred_element_type=F32).astype(BF16)
        at = 0
        for out in outs:
            out[...] = value[at:at + out.shape[0]]
            at += out.shape[0]


def ffn(pieces, out_rows, w_gate, w_up, w_down):
    width, inner = w_gate.shape[1:]
    sizes = [piece.shape[0] for piece in pieces]
    rows = sum(sizes)
    outs = rows // out_rows
    tile = width // STEPS

    def first(i):
        return jnp.minimum(i, STEPS - 1)

    def second(i):
        return jnp.maximum(i - STEPS, 0)

    return pl.pallas_call(
        lambda *refs: ffn_kernel(len(sizes), *refs),
        name="ffn",
        grid=(2 * STEPS,),
        in_specs=[pl.BlockSpec((size, tile), lambda i: (0, first(i))) for size in sizes]
        + [pl.BlockSpec(memory_space=pltpu.VMEM)] * 3,
        out_specs=[pl.BlockSpec((out_rows, tile), lambda i: (0, second(i)))] * outs,
        out_shape=[jax.ShapeDtypeStruct((out_rows, width), BF16)] * outs,
        scratch_shapes=[
            pltpu.VMEM((rows, inner), F32),
            pltpu.VMEM((rows, inner), F32),
            pltpu.VMEM((rows, inner), BF16),
        ],
        cost_estimate=pl.CostEstimate(
            flops=6 * rows * width * inner,
            bytes_accessed=6 * width * inner + 4 * rows * width,
            transcendentals=rows * inner,
        ),
        compiler_params=pltpu.CompilerParams(vmem_limit_bytes=20 * 2**20),
    )(*pieces, w_gate, w_up, w_down)


def layer(tokens, routes, gates, capacity, w_gate, w_up, w_down):
    owner = lax.axis_index("expert")
    rows = tokens.shape[0]
    experts = lax.axis_size("expert")
    slots = 4 * rows // experts
    half = slots // CORES
    core = owner % CORES
    z = owner // CORES
    slot_ids = (core * half + jnp.arange(slots, dtype=jnp.int32)) % slots

    def route(expert):
        matched = routes == expert
        member = jnp.any(matched, axis=-1).astype(jnp.int32)
        weight = jnp.sum(jnp.where(matched, gates, 0.0), axis=-1)
        position = jnp.cumsum(member) - member
        limit = jnp.sum(jnp.where(jnp.arange(experts, dtype=jnp.int32) == expert, capacity, 0))
        kept = (member == 1) & (position < limit)
        picked = kept[None, :] & (position[None, :] == slot_ids[:, None])
        return picked.astype(BF16), weight

    pick_other, weight_other = route(owner + 1 - 2 * core)
    pick_own, weight_own = route(owner)
    block = jnp.dot(
        jnp.concatenate([pick_other[:half], pick_own[:half]], 0), tokens, preferred_element_type=F32
    ).astype(BF16)

    def gather(block):
        near = ring_gather(block, 0)
        line = jnp.concatenate((block,) + near, 0)
        return (line,) + ring_gather(line, 1)

    other = gather(block[:half])
    own = gather(block[half:])
    given = [swap(value) for value in other]
    weights = (w_gate, w_up, w_down)
    q = other[3].shape[0]
    line = ffn([own[0], given[0]], q, *weights)
    near_given = ffn([given[1], given[2]], q, *weights)
    near_own = ffn([own[1], own[2]], q, *weights)
    far = ffn([own[3], own[4], given[3], given[4]], q, *weights)
    back = {}
    for name, values in (("pl", line[2:]), ("pn", near_given), ("pf", far[2:])):
        back[name] = [swap(value) for value in values]

    def scatter(line, near, far):
        return ring_scatter(line, near[:2], near[2:], far, 1)

    width = tokens.shape[1]
    q = half // 2
    minus, plus, near_minus, near_plus, own_sum = vmem_call(
        line_kernel,
        [((4 * q, width), BF16)] * 2 + [((2 * q, width), F32)] * 2 + [((4 * q, width), F32)],
        *scatter(back["pl"], back["pn"], back["pf"]),
        *scatter(line[:2], near_own, far[:2]),
    )
    from_minus = hop(minus, 0, -1)
    from_plus = hop(plus, 0, 1)
    near_after = hop(add(near_minus, from_minus[:2 * q]).astype(BF16), 0, -1)
    near_before = hop(add(near_plus, from_plus[:2 * q]).astype(BF16), 0, 1)

    part = width // experts
    picks = jnp.stack([pick_other.T, pick_own.T])
    weights = jnp.stack([weight_other, weight_own], 1)
    place = jnp.stack([z, core])
    mine, theirs = vmem_call(
        sum_kernel,
        [((slots, SIDE * part), BF16)] * 2,
        place, own_sum, from_minus, from_plus, near_after, near_before,
        scalars=1,
    )
    sums = vmem_call(
        spread_kernel,
        [((rows, part), F32)] + [((rows, part), BF16)] * (SIDE - 1),
        place, mine, swap(theirs), picks, weights,
        scalars=1,
    )
    came = [hop_z(sums[step], step if step < 3 else -1) for step in (2, 1, 3)]
    return vmem_call(final_kernel, [((rows, part), BF16)], sums[0], *came)[0]


def solution(mesh):
    in_specs = (
        P("dp", None),
        P("dp", None),
        P("dp", None),
        P(),
        P("expert", None, "dp"),
        P("expert", None, "dp"),
        P("expert", "dp", None),
    )
    return jax.shard_map(layer, mesh=mesh, in_specs=in_specs, out_specs=P("dp", "expert"), check_vma=False)
```

```python
import jax
import jax.numpy as jnp
from jax import lax
from jax.experimental import pallas as pl
from jax.experimental.pallas import tpu as pltpu
from jax.sharding import PartitionSpec as P


SIDE = 4
CORES = 2
F32 = jnp.float32
BF16 = jnp.bfloat16
STEPS = 4


def move(value, route):
    pairs = []
    for device in range(SIDE * SIDE * SIDE * CORES):
        rest, core = divmod(device, CORES)
        rest, z = divmod(rest, SIDE)
        x, y = divmod(rest, SIDE)
        x, y, z, core = route(x, y, z, core)
        pairs.append((device, ((x % SIDE * SIDE + y % SIDE) * SIDE + z % SIDE) * CORES + core))
    return lax.ppermute(value, ("dp", "expert"), pairs)


def hop(value, leg, step):
    def route(x, y, z, core):
        if core == leg:
            return x + step, y, z, core
        return x, y + step, z, core

    return move(value, route)


def hop_z(value, step):
    return move(value, lambda x, y, z, core: (x, y, z + step, core))


def swap(value):
    return move(value, lambda x, y, z, core: (x, y, z, 1 - core))


def ring_gather(block, leg):
    half = block.shape[0] // 2
    before = hop(block, leg, 1)
    after = hop(block, leg, -1)
    far_low = hop(before[:half], leg, 1)
    far_high = hop(after[half:], leg, -1)
    return before, after, far_low, far_high


def add(first, *others):
    total = first.astype(F32)
    for other in others:
        total = total + other.astype(F32)
    return total


def ring_scatter(own, before, after, far, leg):
    low_after = hop(before[1], leg, -1)
    low_before = hop(after[0], leg, 1)
    low = hop(far[0], leg, -1)
    high = hop(far[1], leg, 1)
    from_after = hop(add(before[0], low).astype(BF16), leg, -1)
    from_before = hop(add(after[1], high).astype(BF16), leg, 1)
    return own[0], low_before, from_after, own[1], low_after, from_before


def vmem_call(kernel, outs, *args, scalars=0, blocks=0, limit=20):
    specs = [pl.BlockSpec(memory_space=pltpu.SMEM)] * scalars
    specs += [pl.BlockSpec(memory_space=pltpu.VMEM)] * (len(args) - scalars - blocks)
    specs += [pl.BlockSpec()] * blocks
    space = pl.BlockSpec(memory_space=pltpu.VMEM) if limit < 50 else pl.BlockSpec()
    return pl.pallas_call(
        kernel,
        in_specs=specs,
        out_specs=[space] * len(outs),
        out_shape=[jax.ShapeDtypeStruct(shape, dtype) for shape, dtype in outs],
        compiler_params=pltpu.CompilerParams(vmem_limit_bytes=limit * 2**20),
    )(*args)


def line_kernel(own_low, low_before, from_after, own_high, low_after, from_before, *outs):
    minus, plus, near_minus, near_plus, own = outs
    tile = 512
    q = near_minus.shape[0]

    @pl.loop(0, minus.shape[1] // tile)
    def _(i):
        at = pl.ds(pl.multiple_of(i * tile, tile), tile)
        low = add(own_low[:, at], low_before[:, at], from_after[:, at])
        high = add(own_high[:, at], low_after[:, at], from_before[:, at])
        own[:, at] = low[:2 * q]
        near_minus[:, at] = low[2 * q:3 * q]
        minus[q:, at] = low[3 * q:].astype(BF16)
        plus[q:, at] = high[:q].astype(BF16)
        near_plus[:, at] = high[q:2 * q]
        minus[:q, at] = high[2 * q:3 * q].astype(BF16)
        plus[:q, at] = high[3 * q:].astype(BF16)


def sum_kernel(place, *refs):
    chains, (mine, theirs) = (refs[:5], refs[5:10]), refs[10:]
    width = mine.shape[1] // SIDE
    q = mine.shape[0] // 4

    @pl.loop(0, SIDE)
    def _(k):
        to = pl.ds(pl.multiple_of(k * width, width), width)
        for core, out in ((place[1], mine), (1 - place[1], theirs)):
            at = pl.ds(pl.multiple_of((CORES * k + core) * width, width), width)
            for n, (own, from_minus, from_plus, near_after, near_before) in enumerate(chains):
                first = add(own[:q, at], from_plus[q:, at], near_after[:, at])
                second = add(own[q:, at], from_minus[q:, at], near_before[:, at])
                rows = pl.ds(2 * n * q, 2 * q)
                out[rows, to] = jnp.concatenate([first, second], 0).astype(BF16)


def spread_kernel(place, mine, theirs, picks, weights, *outs):
    half = mine.shape[0] // 2
    width = outs[0].shape[1]
    for step, out in enumerate(outs):
        at = pl.ds(pl.multiple_of((place[0] + step) % SIDE * width, width), width)
        total = 0.0
        for e in range(2):
            rows = [mine[e * half:(e + 1) * half, at], theirs[(1 - e) * half:(2 - e) * half, at]]
            value = jnp.dot(picks[e], jnp.concatenate(rows, 0), preferred_element_type=F32)
            total = total + weights[:, e:e + 1] * value
        out[...] = total.astype(out.dtype)


def final_kernel(own, *refs):
    refs[-1][...] = add(own[...], *[ref[...] for ref in refs[:-1]]).astype(BF16)


def ffn_kernel(n, *refs):
    pieces, (w_gate, w_up, w_down) = refs[:n], refs[n:n + 3]
    outs, (gate_sum, up_sum, hidden) = refs[n + 3:-3], refs[-3:]
    i = pl.program_id(0)

    @pl.when(i < STEPS)
    def _():
        block = jnp.concatenate([piece[...] for piece in pieces], 0)
        tile = block.shape[1]
        at = pl.ds(pl.multiple_of(i * tile, tile), tile)
        gate_value = jnp.dot(block, w_gate[0, at], preferred_element_type=F32)
        up_value = jnp.dot(block, w_up[0, at], preferred_element_type=F32)

        @pl.when(i == 0)
        def _():
            gate_sum[...] = gate_value
            up_sum[...] = up_value

        @pl.when(i > 0)
        def _():
            gate_sum[...] += gate_value
            up_sum[...] += up_value

        @pl.when(i == STEPS - 1)
        def _():
            hidden[...] = (jax.nn.silu(gate_sum[...]) * up_sum[...]).astype(BF16)

    @pl.when(i >= STEPS)
    def _():
        tile = outs[0].shape[1]
        cols = pl.ds(pl.multiple_of((i - STEPS) * tile, tile), tile)
        value = jnp.dot(hidden[...], w_down[0, :, cols], preferred_element_type=F32).astype(BF16)
        at = 0
        for out in outs:
            out[...] = value[at:at + out.shape[0]]
            at += out.shape[0]


def ffn(pieces, out_rows, w_gate, w_up, w_down):
    width, inner = w_gate.shape[1:]
    sizes = [piece.shape[0] for piece in pieces]
    rows = sum(sizes)
    outs = rows // out_rows
    tile = width // STEPS

    def first(i):
        return jnp.minimum(i, STEPS - 1)

    def second(i):
        return jnp.maximum(i - STEPS, 0)

    return pl.pallas_call(
        lambda *refs: ffn_kernel(len(sizes), *refs),
        name="ffn",
        grid=(2 * STEPS,),
        in_specs=[pl.BlockSpec((size, tile), lambda i: (0, first(i))) for size in sizes]
        + [pl.BlockSpec(memory_space=pltpu.VMEM)] * 3,
        out_specs=[pl.BlockSpec((out_rows, tile), lambda i: (0, second(i)))] * outs,
        out_shape=[jax.ShapeDtypeStruct((out_rows, width), BF16)] * outs,
        scratch_shapes=[
            pltpu.VMEM((rows, inner), F32),
            pltpu.VMEM((rows, inner), F32),
            pltpu.VMEM((rows, inner), BF16),
        ],
        cost_estimate=pl.CostEstimate(
            flops=6 * rows * width * inner,
            bytes_accessed=6 * width * inner + 4 * rows * width,
            transcendentals=rows * inner,
        ),
        compiler_params=pltpu.CompilerParams(vmem_limit_bytes=20 * 2**20),
    )(*pieces, w_gate, w_up, w_down)


def layer(tokens, routes, gates, capacity, w_gate, w_up, w_down):
    owner = lax.axis_index("expert")
    rows = tokens.shape[0]
    experts = lax.axis_size("expert")
    slots = 4 * rows // experts
    half = slots // CORES
    core = owner % CORES
    z = owner // CORES
    slot_ids = (core * half + jnp.arange(slots, dtype=jnp.int32)) % slots

    def route(expert):
        matched = routes == expert
        member = jnp.any(matched, axis=-1).astype(jnp.int32)
        weight = jnp.sum(jnp.where(matched, gates, 0.0), axis=-1)
        position = jnp.cumsum(member) - member
        limit = jnp.sum(jnp.where(jnp.arange(experts, dtype=jnp.int32) == expert, capacity, 0))
        kept = (member == 1) & (position < limit)
        picked = kept[None, :] & (position[None, :] == slot_ids[:, None])
        return picked.astype(BF16), weight

    pick_other, weight_other = route(owner + 1 - 2 * core)
    pick_own, weight_own = route(owner)
    block = jnp.dot(
        jnp.concatenate([pick_other[:half], pick_own[:half]], 0), tokens, preferred_element_type=F32
    ).astype(BF16)

    def gather(block):
        near = ring_gather(block, 0)
        line = jnp.concatenate((block,) + near, 0)
        return (line,) + ring_gather(line, 1)

    other = gather(block[:half])
    own = gather(block[half:])
    given = [swap(value) for value in other]
    weights = (w_gate, w_up, w_down)
    q = other[3].shape[0]
    line = ffn([own[0], given[0]], q, *weights)
    near_given = ffn([given[1], given[2]], q, *weights)
    near_own = ffn([own[1], own[2]], q, *weights)
    far = ffn([own[3], own[4], given[3], given[4]], q, *weights)
    back = {}
    for name, values in (("pl", line[2:]), ("pn", near_given), ("pf", far[2:])):
        back[name] = [swap(value) for value in values]

    def scatter(line, near, far):
        return ring_scatter(line, near[:2], near[2:], far, 1)

    width = tokens.shape[1]
    q = half // 2

    def second_leg(terms):
        minus, plus, near_minus, near_plus, own_sum = vmem_call(
            line_kernel,
            [((2 * q, width), BF16)] * 2 + [((q, width), F32)] * 2 + [((2 * q, width), F32)],
            *terms,
        )
        from_minus = hop(minus, 0, -1)
        from_plus = hop(plus, 0, 1)
        near_after = hop(add(near_minus, from_minus[:q]).astype(BF16), 0, -1)
        near_before = hop(add(near_plus, from_plus[:q]).astype(BF16), 0, 1)
        return own_sum, from_minus, from_plus, near_after, near_before

    own_terms = second_leg(scatter(line[:2], near_own, far[:2]))
    other_terms = second_leg(scatter(back["pl"], back["pn"], back["pf"]))

    part = width // experts
    picks = jnp.stack([pick_other.T, pick_own.T])
    weights = jnp.stack([weight_other, weight_own], 1)
    place = jnp.stack([z, core])
    mine, theirs = vmem_call(
        sum_kernel,
        [((slots, SIDE * part), BF16)] * 2,
        place, *other_terms, *own_terms,
        scalars=1,
    )
    sums = vmem_call(
        spread_kernel,
        [((rows, part), F32)] + [((rows, part), BF16)] * (SIDE - 1),
        place, mine, swap(theirs), picks, weights,
        scalars=1,
    )
    came = [hop_z(sums[step], step if step < 3 else -1) for step in (2, 1, 3)]
    return vmem_call(final_kernel, [((rows, part), BF16)], sums[0], *came)[0]


def solution(mesh):
    in_specs = (
        P("dp", None),
        P("dp", None),
        P("dp", None),
        P(),
        P("expert", None, "dp"),
        P("expert", None, "dp"),
        P("expert", "dp", None),
    )
    return jax.shard_map(
        layer, mesh=mesh, in_specs=in_specs, out_specs=P("dp", "expert"), check_vma=False
    )
```

```python
import jax
import jax.numpy as jnp
from jax import lax
from jax.experimental import pallas as pl
from jax.experimental.pallas import tpu as pltpu
from jax.sharding import PartitionSpec as P


SIDE = 4
CORES = 2
F32 = jnp.float32
BF16 = jnp.bfloat16
STEPS = 4


def move(value, route):
    pairs = []
    for device in range(SIDE * SIDE * SIDE * CORES):
        rest, core = divmod(device, CORES)
        rest, z = divmod(rest, SIDE)
        x, y = divmod(rest, SIDE)
        x, y, z, core = route(x, y, z, core)
        pairs.append((device, ((x % SIDE * SIDE + y % SIDE) * SIDE + z % SIDE) * CORES + core))
    return lax.ppermute(value, ("dp", "expert"), pairs)


def hop(value, leg, step):
    def route(x, y, z, core):
        if core == leg:
            return x + step, y, z, core
        return x, y + step, z, core

    return move(value, route)


def hop_z(value, step):
    return move(value, lambda x, y, z, core: (x, y, z + step, core))


def swap(value):
    return move(value, lambda x, y, z, core: (x, y, z, 1 - core))


def ring_gather(block, leg):
    half = block.shape[0] // 2
    before = hop(block, leg, 1)
    after = hop(block, leg, -1)
    far_low = hop(before[:half], leg, 1)
    far_high = hop(after[half:], leg, -1)
    return before, after, far_low, far_high


def add(first, *others):
    total = first.astype(F32)
    for other in others:
        total = total + other.astype(F32)
    return total


def ring_scatter(own, before, after, far, leg):
    low_after = hop(before[1], leg, -1)
    low_before = hop(after[0], leg, 1)
    low = hop(far[0], leg, -1)
    high = hop(far[1], leg, 1)
    from_after = hop(add(before[0], low).astype(BF16), leg, -1)
    from_before = hop(add(after[1], high).astype(BF16), leg, 1)
    return own[0], low_before, from_after, own[1], low_after, from_before


def vmem_call(kernel, outs, *args, scalars=0, blocks=0, limit=20):
    specs = [pl.BlockSpec(memory_space=pltpu.SMEM)] * scalars
    specs += [pl.BlockSpec(memory_space=pltpu.VMEM)] * (len(args) - scalars - blocks)
    specs += [pl.BlockSpec()] * blocks
    space = pl.BlockSpec(memory_space=pltpu.VMEM) if limit < 50 else pl.BlockSpec()
    return pl.pallas_call(
        kernel,
        in_specs=specs,
        out_specs=[space] * len(outs),
        out_shape=[jax.ShapeDtypeStruct(shape, dtype) for shape, dtype in outs],
        compiler_params=pltpu.CompilerParams(vmem_limit_bytes=limit * 2**20),
    )(*args)


def line_kernel(own_low, low_before, from_after, own_high, low_after, from_before, *outs):
    minus, plus, near_minus, near_plus, own = outs
    tile = 512
    q = near_minus.shape[0]

    @pl.loop(0, minus.shape[1] // tile)
    def _(i):
        at = pl.ds(pl.multiple_of(i * tile, tile), tile)
        low = add(own_low[:, at], low_before[:, at], from_after[:, at])
        high = add(own_high[:, at], low_after[:, at], from_before[:, at])
        own[:, at] = low[:2 * q]
        near_minus[:, at] = low[2 * q:3 * q]
        minus[q:, at] = low[3 * q:].astype(BF16)
        plus[q:, at] = high[:q].astype(BF16)
        near_plus[:, at] = high[q:2 * q]
        minus[:q, at] = high[2 * q:3 * q].astype(BF16)
        plus[:q, at] = high[3 * q:].astype(BF16)


def sum_kernel(place, *refs):
    chains, (mine, theirs) = (refs[:5], refs[5:10]), refs[10:]
    width = mine.shape[1] // SIDE
    q = mine.shape[0] // 4

    @pl.loop(0, SIDE)
    def _(k):
        to = pl.ds(pl.multiple_of(k * width, width), width)
        for core, out in ((place[1], mine), (1 - place[1], theirs)):
            at = pl.ds(pl.multiple_of((CORES * k + core) * width, width), width)
            for n, (own, from_minus, from_plus, near_after, near_before) in enumerate(chains):
                first = add(own[:q, at], from_plus[q:, at], near_after[:, at])
                second = add(own[q:, at], from_minus[q:, at], near_before[:, at])
                rows = pl.ds(2 * n * q, 2 * q)
                out[rows, to] = jnp.concatenate([first, second], 0).astype(BF16)


def spread_kernel(place, mine, theirs, picks, weights, *outs):
    half = mine.shape[0] // 2
    width = outs[0].shape[1]
    for step, out in enumerate(outs):
        at = pl.ds(pl.multiple_of((place[0] + step) % SIDE * width, width), width)
        total = 0.0
        for e in range(2):
            rows = [mine[e * half:(e + 1) * half, at], theirs[(1 - e) * half:(2 - e) * half, at]]
            value = jnp.dot(picks[e], jnp.concatenate(rows, 0), preferred_element_type=F32)
            total = total + weights[:, e:e + 1] * value
        out[...] = total.astype(out.dtype)


def final_kernel(own, *refs):
    refs[-1][...] = add(own[...], *[ref[...] for ref in refs[:-1]]).astype(BF16)


def ffn_kernel(n, *refs):
    pieces, (w_gate, w_up, w_down) = refs[:n], refs[n:n + 3]
    outs, (gate_sum, up_sum, hidden) = refs[n + 3:-3], refs[-3:]
    i = pl.program_id(0)

    @pl.when(i < STEPS)
    def _():
        block = jnp.concatenate([piece[...] for piece in pieces], 0)
        tile = block.shape[1]
        at = pl.ds(pl.multiple_of(i * tile, tile), tile)
        gate_value = jnp.dot(block, w_gate[0, at], preferred_element_type=F32)
        up_value = jnp.dot(block, w_up[0, at], preferred_element_type=F32)

        @pl.when(i == 0)
        def _():
            gate_sum[...] = gate_value
            up_sum[...] = up_value

        @pl.when(i > 0)
        def _():
            gate_sum[...] += gate_value
            up_sum[...] += up_value

        @pl.when(i == STEPS - 1)
        def _():
            hidden[...] = (jax.nn.silu(gate_sum[...]) * up_sum[...]).astype(BF16)

    @pl.when(i >= STEPS)
    def _():
        tile = outs[0].shape[1]
        cols = pl.ds(pl.multiple_of((i - STEPS) * tile, tile), tile)
        value = jnp.dot(hidden[...], w_down[0, :, cols], preferred_element_type=F32).astype(BF16)
        at = 0
        for out in outs:
            out[...] = value[at:at + out.shape[0]]
            at += out.shape[0]


def ffn(pieces, out_rows, w_gate, w_up, w_down):
    width, inner = w_gate.shape[1:]
    sizes = [piece.shape[0] for piece in pieces]
    rows = sum(sizes)
    outs = rows // out_rows
    tile = width // STEPS

    def first(i):
        return jnp.minimum(i, STEPS - 1)

    def second(i):
        return jnp.maximum(i - STEPS, 0)

    return pl.pallas_call(
        lambda *refs: ffn_kernel(len(sizes), *refs),
        name="ffn",
        grid=(2 * STEPS,),
        in_specs=[pl.BlockSpec((size, tile), lambda i: (0, first(i))) for size in sizes]
        + [pl.BlockSpec(memory_space=pltpu.VMEM)] * 3,
        out_specs=[pl.BlockSpec((out_rows, tile), lambda i: (0, second(i)))] * outs,
        out_shape=[jax.ShapeDtypeStruct((out_rows, width), BF16)] * outs,
        scratch_shapes=[
            pltpu.VMEM((rows, inner), F32),
            pltpu.VMEM((rows, inner), F32),
            pltpu.VMEM((rows, inner), BF16),
        ],
        cost_estimate=pl.CostEstimate(
            flops=6 * rows * width * inner,
            bytes_accessed=6 * width * inner + 4 * rows * width,
            transcendentals=rows * inner,
        ),
        compiler_params=pltpu.CompilerParams(vmem_limit_bytes=20 * 2**20),
    )(*pieces, w_gate, w_up, w_down)


def layer(tokens, routes, gates, capacity, w_gate, w_up, w_down):
    owner = lax.axis_index("expert")
    rows = tokens.shape[0]
    experts = lax.axis_size("expert")
    slots = 4 * rows // experts
    half = slots // CORES
    core = owner % CORES
    z = owner // CORES
    slot_ids = (core * half + jnp.arange(slots, dtype=jnp.int32)) % slots

    def route(expert):
        matched = routes == expert
        member = jnp.any(matched, axis=-1).astype(jnp.int32)
        weight = jnp.sum(jnp.where(matched, gates, 0.0), axis=-1)
        position = jnp.cumsum(member) - member
        ids = jnp.arange(experts, dtype=jnp.int32)
        named = (routes[:, :, None] == ids) & (ids == expert)
        limit = jnp.sum(jnp.where(named, capacity, 0), axis=(1, 2))
        kept = position < limit
        picked = kept[None, :] & (position[None, :] == slot_ids[:, None])
        return picked.astype(BF16), weight

    pick_other, weight_other = route(owner + 1 - 2 * core)
    pick_own, weight_own = route(owner)
    block = jnp.dot(
        jnp.concatenate([pick_other[:half], pick_own[:half]], 0), tokens, preferred_element_type=F32
    ).astype(BF16)

    def gather(block):
        near = ring_gather(block, 0)
        line = jnp.concatenate((block,) + near, 0)
        return (line,) + ring_gather(line, 1)

    other = gather(block[:half])
    own = gather(block[half:])
    given = [swap(value) for value in other]
    weights = (w_gate, w_up, w_down)
    q = other[3].shape[0]
    line = ffn([own[0], given[0]], q, *weights)
    near_given = ffn([given[1], given[2]], q, *weights)
    near_own = ffn([own[1], own[2]], q, *weights)
    far = ffn([own[3], own[4], given[3], given[4]], q, *weights)
    back = {}
    for name, values in (("pl", line[2:]), ("pn", near_given), ("pf", far[2:])):
        back[name] = [swap(value) for value in values]

    def scatter(line, near, far):
        return ring_scatter(line, near[:2], near[2:], far, 1)

    width = tokens.shape[1]
    q = half // 2

    def second_leg(terms):
        minus, plus, near_minus, near_plus, own_sum = vmem_call(
            line_kernel,
            [((2 * q, width), BF16)] * 2 + [((q, width), F32)] * 2 + [((2 * q, width), F32)],
            *terms,
        )
        from_minus = hop(minus, 0, -1)
        from_plus = hop(plus, 0, 1)
        near_after = hop(add(near_minus, from_minus[:q]).astype(BF16), 0, -1)
        near_before = hop(add(near_plus, from_plus[:q]).astype(BF16), 0, 1)
        return own_sum, from_minus, from_plus, near_after, near_before

    own_terms = second_leg(scatter(line[:2], near_own, far[:2]))
    other_terms = second_leg(scatter(back["pl"], back["pn"], back["pf"]))

    part = width // experts
    picks = jnp.stack([pick_other.T, pick_own.T])
    weights = jnp.stack([weight_other, weight_own], 1)
    place = jnp.stack([z, core])
    mine, theirs = vmem_call(
        sum_kernel,
        [((slots, SIDE * part), BF16)] * 2,
        place, *other_terms, *own_terms,
        scalars=1,
    )
    sums = vmem_call(
        spread_kernel,
        [((rows, part), F32)] + [((rows, part), BF16)] * (SIDE - 1),
        place, mine, swap(theirs), picks, weights,
        scalars=1,
    )
    came = [hop_z(sums[step], step if step < 3 else -1) for step in (2, 1, 3)]
    return vmem_call(final_kernel, [((rows, part), BF16)], sums[0], *came)[0]


def solution(mesh):
    in_specs = (
        P("dp", None),
        P("dp", None),
        P("dp", None),
        P(),
        P("expert", None, "dp"),
        P("expert", None, "dp"),
        P("expert", "dp", None),
    )
    return jax.shard_map(
        layer, mesh=mesh, in_specs=in_specs, out_specs=P("dp", "expert"), check_vma=False
    )
```
